32 devices in a mesh: groups: 2 (over x), section: 1, expert: 16 (over z, y, core).
Axes of the slice: x: 2, y: 2, z: 4, core: 2. Of those that a mesh axis runs over, the one named last changes fastest.
Arguments:
- inputs: bfloat16 [2, 512, 2048], P(None, ('groups', 'expert')), parts along dimension 1, may hold values from -6 to 6
- routes: int32 [2, 2, 512, 8], P('section', None, ('groups', 'expert')), parts along dimension 2, may hold values from 0 to 15, all different within a row; in each aligned block of 16 rows (0 to 15, 16 to 31, ..., all dimensions but the last counted through in order) at most 16 rows name the same one
- norm_gain: float32 [2, 2048], P('section'), may hold values from 0.1 to 1.9
- w_gate_up: bfloat16 [2, 16, 2048, 1536], P('section', 'expert'), may hold values from -0.125 to 0.125
- w_down: bfloat16 [2, 16, 768, 2048], P('section', 'expert'), may hold values from -0.4375 to 0.4375
Outputs:
- outputs: bfloat16 [2, 2, 512, 2048], P('section', None, ('groups', 'expert')), parts along dimension 2
The draws below stay inside these ranges and needn't reach their ends.
There are 2 independent parts, one for each index of `groups`. The reference program is written for one: setup_inputs(seed, part) draws one part's arguments, and reference() takes and returns one part's arrays. A program takes and returns all parts, laid end to end along the dimension named above; an argument that names none is the same for every part. Nothing has to cross between parts.
Inputs may be any that keep to these rules, and one draw needn't show every extreme that they name: `routes`: the 8 entries of a row differ. In each aligned block of 16 rows (the rows of one index of expert in one micro-batch of one layer) no expert is named by more than 16 rows, and some block reaches 16.
All inputs are finite; a program needn't handle non-finite values.
Results may differ from the reference program's by a relative error of at most 0.0055.
Values may be sent and summed in bfloat16 or wider, within the bound.
A program may use at most 64 MiB of HBM per device.

```python
import math
import jax
import jax.numpy as jnp
import numpy as np
from jax import lax

D = 2048
F = 768
TOP = 8
MB = 2
TOK_MB = 16
EXPERTS = 16
TOKENS = 256
CAP = 16


def block_levels(own_key, extent, cuts, least, largest):
    level = 1.0
    for position, shards_of in cuts:
        steps = jax.random.uniform(jax.random.fold_in(jax.random.fold_in(own_key, 6), position), (shards_of,), jnp.float32, least / len(cuts), largest / len(cuts))
        level = level * jnp.repeat(jnp.exp(steps), extent[position] // shards_of).reshape((-1,) + (1,) * (len(extent) - 1 - position))
    return level


def deal_out(stream_key, own, number, rows, number_of, top, most, skew):
    order = jax.random.permutation(stream_key, number_of)
    crowded, usual = load_shares(number_of, rows * top, most, skew, True), load_shares(number_of, rows * top, most, skew, False)
    places = jnp.arange(number_of)

    def named(tallies, rotation):
        used = int((tallies > 0).sum())
        fixed = max(1, used // 4)
        moved = fixed + (places - fixed + rotation * (used - fixed)) % max(1, number_of - fixed)
        return jnp.zeros((number_of,), jnp.int32).at[order[jnp.where(places < fixed, places, moved)]].set(jnp.asarray(tallies, jnp.int32))

    tallies = jnp.where(number % 4 == 0, named(crowded, number // 4), named(usual, number - number // 4 - 1))
    mixed = jax.random.permutation(jax.random.fold_in(own, 3), number_of)
    giver, sink = mixed[0:number_of // 2 * 2:2], mixed[1:number_of // 2 * 2:2]
    slack = jnp.minimum(tallies[giver] - 1, most - tallies[sink]) // 2
    slack = jnp.where((giver == order[0]) | (sink == order[0]) | (tallies[sink] == 0), 0, jnp.maximum(slack, 0))
    moved = jax.random.randint(jax.random.fold_in(own, 4), (number_of // 2,), 0, 1 << 20) % (slack + 1)
    tallies = tallies.at[giver].add(-moved).at[sink].add(moved)
    items = jnp.searchsorted(jnp.cumsum(tallies), jnp.arange(rows * top), side="right").astype(jnp.int32)
    listing = items.reshape(top, rows).T
    listing = listing[jax.random.permutation(jax.random.fold_in(own, 1), rows)]
    rotation = jax.random.randint(jax.random.fold_in(own, 2), (rows, 1), 0, top)
    return jnp.take_along_axis(listing, (jnp.arange(top)[None, :] + rotation) % top, axis=1)


def load_shares(amount, total, most, skew, full):
    weights = [(1 << 20) // math.isqrt(grade ** skew) + 1 for grade in range(1, amount + 1)]
    largest = most if full else min(most, max(-(-total // amount), total * weights[0] // sum(weights)))
    least = 1 if total - largest >= amount - 1 else 0
    given, spare = [largest] + [least] * (amount - 1), total - largest - least * (amount - 1)
    while spare > 0:
        candidates = [i for i in range(1, amount) if given[i] < largest] or [i for i in range(1, amount) if given[i] < most]
        pool, budget = sum([weights[i] for i in candidates]), spare
        for i in candidates:
            addition = min(most - given[i], max(1, budget * weights[i] // pool), spare)
            given[i] = given[i] + addition
            spare = spare - addition
    return np.array(given)


def gaussian(stream_key, extent, deviation, bound, split=(), held_as=jnp.bfloat16):
    level = block_levels(stream_key, extent, split, -0.22, 0.18) if split else 1.0
    drawn = jax.random.normal(stream_key, extent, jnp.float32) * deviation * level
    return jnp.minimum(jnp.maximum(drawn, -bound), bound).astype(held_as)


def setup_inputs(seed: int = 0, part: int = 0) -> dict:
    splits = jax.random.split(jax.random.key(seed), 6)
    part_splits = jax.random.split(jax.random.fold_in(splits[5], part), 6)
    inputs = gaussian(part_splits[0], (MB, TOKENS, D), 1.0, 6.0, ((1, 16),))
    routes_keys = jax.random.split(jax.random.fold_in(part_splits[1], 1), 2 * MB * TOKENS // TOK_MB)
    routes_turns = jax.random.permutation(jax.random.fold_in(part_splits[1], 3), 2 * MB * TOKENS // TOK_MB)
    routes = jax.vmap(lambda own, number: deal_out(jax.random.fold_in(part_splits[1], 2), own, number, TOK_MB, EXPERTS, TOP, CAP, 2))(routes_keys, routes_turns).reshape((2, MB, TOKENS, TOP))
    norm_gain = jnp.clip(1.0 + 0.18 * jax.random.normal(splits[2], (2, D), jnp.float32), 0.1, 1.9)
    w_gate_up = gaussian(splits[3], (2, EXPERTS, D, 2 * F), D ** -0.5, 0.125, ((1, 16),))
    w_down = gaussian(splits[4], (2, EXPERTS, F, D), (F // 4) ** -0.5, 0.4375, ((1, 16),))
    return dict(inputs=inputs, routes=routes, norm_gain=norm_gain, w_gate_up=w_gate_up, w_down=w_down)


eps = 1e-06

def expert_ffn(rows, gate_up, down_proj):
    joined = jnp.dot(rows.astype(jnp.float32), gate_up.astype(jnp.float32))
    hidden = (jax.nn.silu(joined[:, :F]) * joined[:, F:]).astype(jnp.bfloat16)
    return jnp.dot(hidden.astype(jnp.float32), down_proj.astype(jnp.float32)).astype(jnp.bfloat16)

def moe_layer(current, layer_routes, gain_row, gate_up, down_proj):
    widened = current.astype(jnp.float32)
    scale_inv = lax.rsqrt(lax.optimization_barrier(jnp.mean(widened * widened, axis=-1, keepdims=True)) + eps)
    normed = (widened * scale_inv * gain_row).astype(jnp.bfloat16)
    flat_routes = layer_routes.reshape(-1).astype(jnp.int32)
    expert_ids = jnp.arange(EXPERTS, dtype=jnp.int32)
    onehot = (flat_routes[:, None] == expert_ids[None, :]).astype(jnp.int32)
    before = jnp.cumsum(onehot, axis=0) - onehot
    rank_of = lax.optimization_barrier(jnp.sum(before * onehot, axis=1))
    room = EXPERTS * CAP
    target = (flat_routes * room + rank_of).astype(jnp.int32)
    source = jnp.repeat(normed, TOP, axis=0)
    buffer = jnp.zeros((EXPERTS * room, D), jnp.bfloat16).at[target].set(source)
    results = lax.map(lambda packed: expert_ffn(packed[0], packed[1], packed[2]), (buffer.reshape(EXPERTS, room, D), gate_up, down_proj))
    picked = results.reshape(EXPERTS * room, D)[target].reshape(TOKENS, TOP, D).astype(jnp.float32)
    combined = lax.optimization_barrier(jnp.sum(picked, axis=1)) * 0.125
    return (widened + combined).astype(jnp.bfloat16)

def reference(inputs, routes, norm_gain, w_gate_up, w_down):
    first_layer = []
    for batch_no in range(MB):
        first_layer.append(moe_layer(inputs[batch_no], routes[0, batch_no], norm_gain[0], w_gate_up[0], w_down[0]))
    second_layer = []
    for batch_no in range(MB):
        second_layer.append(moe_layer(first_layer[batch_no], routes[1, batch_no], norm_gain[1], w_gate_up[1], w_down[1]))
    return jnp.stack([jnp.stack(first_layer), jnp.stack(second_layer)])
```

```python
import functools

import jax
import jax.numpy as jnp
from jax import lax
from jax.experimental import pallas as pl
from jax.experimental.pallas import tpu as pltpu
from jax.sharding import PartitionSpec as P

eps = 1e-06


def from_behind(value, axis, steps):
    count = lax.axis_size(axis)
    initial, last = (max(0, -steps), min(count, count - steps))
    return lax.ppermute(value, axis, [(source, source + steps) for source in range(initial, last)])


def expert_rows(rows, gate_up, down_proj):
    hidden_size = down_proj.shape[0]
    joined = jnp.dot(rows, gate_up, preferred_element_type=jnp.float32)
    hidden = (jax.nn.silu(joined[:, :hidden_size]) * joined[:, hidden_size:]).astype(jnp.bfloat16)
    return jnp.dot(hidden, down_proj, preferred_element_type=jnp.float32).astype(jnp.bfloat16)


def run_experts(received, gate_up, down_proj):
    flat = received.reshape(-1, received.shape[2])
    done = expert_rows(flat, gate_up, down_proj)
    return done.reshape(received.shape)


def moe_layer(current, layer_routes, gain_row, gate_up, down_proj, experts, capacity):
    tokens, features = current.shape
    widened = current.astype(jnp.float32)
    scale_inv = lax.rsqrt(jnp.mean(widened * widened, axis=-1, keepdims=True) + eps)
    normed = (widened * scale_inv * gain_row).astype(jnp.bfloat16)
    expert_ids = jnp.arange(experts, dtype=jnp.int32)
    onehot = (layer_routes[:, :, None] == expert_ids[None, None, :]).astype(jnp.int32)
    counted = jnp.sum(onehot, axis=1)
    before = jnp.cumsum(counted, axis=0) - counted
    slot_of = jnp.sum(onehot * (expert_ids[None, None, :] * capacity + before[:, None, :]), axis=2)
    slot_ids = jnp.arange(experts * capacity, dtype=jnp.int32)
    placing = jnp.sum(
        (slot_ids[:, None, None] == slot_of[None, :, :]).astype(jnp.int32), axis=2
    ).astype(jnp.bfloat16)
    outgoing = jnp.dot(placing, normed, preferred_element_type=jnp.float32).astype(jnp.bfloat16)
    outgoing = outgoing.reshape(experts, capacity, features)
    results = run_experts(
        lax.all_to_all(outgoing, "expert", split_axis=0, concat_axis=0, tiled=True),
        gate_up,
        down_proj,
    )
    returned = lax.all_to_all(results, "expert", split_axis=0, concat_axis=0, tiled=True).reshape(
        experts * capacity, features
    )
    combined = (
        jnp.einsum("it,id->td", placing, returned, preferred_element_type=jnp.float32) * 0.125
    )
    return (widened + combined).astype(jnp.bfloat16)


def on_device(inputs, routes, norm_gain, w_gate_up, w_down):
    experts = lax.axis_size("expert")
    sections = lax.axis_size("section")
    batches, tokens, features = inputs.shape
    top_k = routes.shape[3]
    capacity = min(tokens, 2 * tokens * top_k // experts)
    if sections == 1:
        layers_out = []
        previous = [inputs[batch_no] for batch_no in range(batches)]
        for layer_no in range(routes.shape[0]):
            current_layer = []
            for batch_no in range(batches):
                current_layer.append(
                    moe_layer(
                        previous[batch_no],
                        routes[layer_no, batch_no],
                        norm_gain[layer_no],
                        w_gate_up[layer_no, 0],
                        w_down[layer_no, 0],
                        experts,
                        capacity,
                    )
                )
            layers_out.append(jnp.stack(current_layer))
            previous = current_layer
        return jnp.stack(layers_out)
    segment_no = lax.axis_index("section")
    layer_routes = routes[0]
    gain_row = norm_gain[0]
    gate_up = w_gate_up[0, 0]
    down_proj = w_down[0, 0]
    handed = jnp.zeros((tokens, features), jnp.bfloat16)
    finished = []
    for turn_no in range(batches + 1):
        if turn_no < batches:
            fresh_rows = inputs[turn_no]
        else:
            fresh_rows = jnp.zeros((tokens, features), jnp.bfloat16)
        current = jnp.where(segment_no == 0, fresh_rows, handed)
        batch_pick = jnp.clip(turn_no - segment_no, 0, batches - 1)
        turn_routes = lax.dynamic_index_in_dim(layer_routes, batch_pick, 0, keepdims=False)
        result = moe_layer(current, turn_routes, gain_row, gate_up, down_proj, experts, capacity)
        finished.append(result)
        if turn_no < batches:
            handed = from_behind(result, "section", 1)
    first_segment = jnp.stack(finished[:batches])
    second_segment = jnp.stack(finished[1:])
    return jnp.where(segment_no == 0, first_segment, second_segment)[None]

LANES = 128
PAIR = 2
TILE = 256


def flat_rows(block):
    return block.reshape(-1, block.shape[-1])


def moe_kernel(
    count,
    x_ref,
    routes_ref,
    gain_ref,
    gu_hbm,
    down_hbm,
    out_ref,
    gu,
    down,
    rows,
    hidden,
    made,
    from_core,
    to_y,
    from_y,
    to_z,
    from_z,
    w_sem,
    az_s,
    az_r,
    ay_s,
    ay_r,
    ac_s,
    ac_r,
    rc_s,
    rc_r,
    ry_s,
    ry_r,
    rz_s,
    rz_r,
):
    layers, batches = routes_ref.shape[0], routes_ref.shape[1]
    tokens, features = x_ref.shape[1], x_ref.shape[2]
    units = down.shape[1]
    depth = count // (PAIR * PAIR)
    me = lax.axis_index("expert")
    c = lax.rem(me, PAIR)
    y = lax.rem(lax.div(me, PAIR), PAIR)
    z = lax.div(me, PAIR * PAIR)
    other_c, other_y = 1 - c, 1 - y

    def expert_at(zz, yy, cc):
        return (zz * PAIR + yy) * PAIR + cc

    def z_up(k):
        return lax.rem(z + k, depth)

    def z_down(k):
        return lax.rem(z + depth - k, depth)

    core_peer = expert_at(z, y, other_c)
    y_peer = expert_at(z, other_y, c)

    def remote(src, dst, send, recv, target):
        return pltpu.make_async_remote_copy(
            src_ref=src,
            dst_ref=dst,
            send_sem=send,
            recv_sem=recv,
            device_id={"expert": target},
            device_id_type=pl.DeviceIdType.MESH,
        )

    loads = []
    for layer in range(layers):
        for number, (source, target) in enumerate(((gu_hbm, gu), (down_hbm, down))):
            load = pltpu.make_async_copy(
                source.at[layer, 0], target.at[layer], w_sem.at[layer, number]
            )
            load.start()
            loads.append(load)

    barrier = pltpu.get_barrier_semaphore()
    for peer in [expert_at(z_up(k), y, c) for k in range(1, depth)] + [core_peer, y_peer]:
        pl.semaphore_signal(
            barrier, inc=1, device_id={"expert": peer}, device_id_type=pl.DeviceIdType.MESH
        )
    pl.semaphore_wait(barrier, depth + 1)

    sends = []

    def go(copy):
        copy.start()
        sends.append(copy)

    def slot(layer, batch):
        return layer * batches + batch

    def gather_core(s, yy, zz, number):
        block = rows.at[s, c, yy, zz]
        return remote(block, block, ac_s.at[s, number], ac_r.at[s, number], core_peer)

    def gather_y(s, zz, number):
        block = rows.at[s, c, y, zz]
        return remote(block, block, ay_s.at[s, number], ay_r.at[s, number], y_peer)

    def norm_send(layer, batch):
        s = slot(layer, batch)
        h = (x_ref[batch] if layer == 0 else out_ref[layer - 1, batch]).astype(jnp.float32)
        scale = lax.rsqrt(jnp.mean(h * h, axis=-1, keepdims=True) + eps)
        normed = (h * scale * gain_ref[pl.ds(layer, 1), :]).astype(jnp.bfloat16)
        rows[s, c, y, z, :, pl.ds(0, features)] = normed
        lanes = lax.broadcasted_iota(jnp.int32, (tokens, LANES), 1)
        chosen = routes_ref[layer, batch]
        named = jnp.zeros((tokens, LANES), jnp.float32)
        for k in range(chosen.shape[1]):
            named = named + (chosen[:, k : k + 1] == lanes).astype(jnp.float32)
        rows[s, c, y, z, :, pl.ds(features, LANES)] = named.astype(jnp.bfloat16)
        block = rows.at[s, c, y, z]
        for k in range(1, depth):
            go(remote(block, block, az_s.at[s, k - 1], az_r.at[s, k - 1], expert_at(z_up(k), y, c)))
        go(gather_y(s, z, 0))
        go(gather_core(s, y, z, 0))

    def gather_z_done(layer, batch):
        s = slot(layer, batch)
        for k in range(1, depth):
            zz = z_down(k)
            block = rows.at[s, c, y, zz]
            remote(block, block, az_s.at[s, k - 1], az_r.at[s, k - 1], y_peer).wait_recv()
            go(gather_y(s, zz, k))
            go(gather_core(s, y, zz, k))

    def gather_y_done(layer, batch):
        s = slot(layer, batch)
        for k in range(depth):
            zz = z_down(k)
            block = rows.at[s, c, other_y, zz]
            remote(block, block, ay_s.at[s, k], ay_r.at[s, k], y_peer).wait_recv()
            go(gather_core(s, other_y, zz, depth + k))

    def gather_core_done(layer, batch):
        s = slot(layer, batch)
        for number in range(PAIR * depth):
            zz = z_down(number % depth)
            block = rows.at[s, other_c, y if number < depth else other_y, zz]
            remote(block, block, ac_s.at[s, number], ac_r.at[s, number], core_peer).wait_recv()

    def compute(layer, batch):
        s = slot(layer, batch)
        if batch == 0:
            for load in loads[layer * 2 : layer * 2 + 2]:
                load.wait()
        named = flat_rows(rows[s, :, :, :, :, pl.ds(features, LANES)]).astype(jnp.float32)
        lanes = lax.broadcasted_iota(jnp.int32, named.shape, 1)
        mine = jnp.sum(jnp.where(lanes == me, named, 0.0), axis=1, keepdims=True) > 0.5

        def up_tile(j, carry):
            gate_cols = pl.ds(pl.multiple_of(j * TILE, TILE), TILE)
            up_cols = pl.ds(pl.multiple_of(units + j * TILE, TILE), TILE)
            x = flat_rows(rows[s, :, :, :, :, pl.ds(0, features)])
            gate = jnp.dot(x, gu[layer, :, gate_cols], preferred_element_type=jnp.float32)
            up = jnp.dot(x, gu[layer, :, up_cols], preferred_element_type=jnp.float32)
            value = gate / (1.0 + jnp.exp(-gate)) * up
            hidden[:, gate_cols] = jnp.where(mine, value, 0.0).astype(jnp.bfloat16)
            return carry

        lax.fori_loop(0, units // TILE, up_tile, 0)

        def down_tile(j, carry):
            cols = pl.ds(pl.multiple_of(j * TILE, TILE), TILE)
            result = jnp.dot(hidden[...], down[layer, :, cols], preferred_element_type=jnp.float32)
            made[s, :, :, :, :, cols] = result.astype(jnp.bfloat16).reshape(
                PAIR, PAIR, depth, tokens, TILE
            )
            return carry

        lax.fori_loop(0, features // TILE, down_tile, 0)

    def sum_core_copy(s, yy, number):
        return remote(
            made.at[s, other_c, yy],
            from_core.at[s, yy],
            rc_s.at[s, number],
            rc_r.at[s, number],
            core_peer,
        )

    def sum_core(layer, batch):
        s = slot(layer, batch)
        go(sum_core_copy(s, other_y, 0))
        go(sum_core_copy(s, y, 1))

    def sum_core_wait(s, yy, number):
        block = from_core.at[s, yy]
        remote(block, block, rc_s.at[s, number], rc_r.at[s, number], core_peer).wait_recv()

    def pair_sum(s, yy, zz):
        return made[s, c, yy, zz].astype(jnp.float32) + from_core[s, yy, zz].astype(jnp.float32)

    def sum_y(layer, batch):
        s = slot(layer, batch)
        sum_core_wait(s, other_y, 0)
        for k in list(range(1, depth)) + [0]:
            zz = z_up(k)
            to_y[s, k] = pair_sum(s, other_y, zz).astype(jnp.bfloat16)
            go(remote(to_y.at[s, k], from_y.at[s, k], ry_s.at[s, k], ry_r.at[s, k], y_peer))

    def sum_y_wait(s, k):
        remote(from_y.at[s, k], from_y.at[s, k], ry_s.at[s, k], ry_r.at[s, k], y_peer).wait_recv()

    def sum_z(layer, batch):
        s = slot(layer, batch)
        sum_core_wait(s, y, 1)
        for k in range(1, depth):
            zz = z_up(k)
            sum_y_wait(s, k)
            total = pair_sum(s, y, zz) + from_y[s, k].astype(jnp.float32)
            to_z[s, k - 1] = total.astype(jnp.bfloat16)
            go(
                remote(
                    to_z.at[s, k - 1],
                    from_z.at[s, k - 1],
                    rz_s.at[s, k - 1],
                    rz_r.at[s, k - 1],
                    expert_at(zz, y, c),
                )
            )

    def finish(layer, batch):
        s = slot(layer, batch)
        sum_y_wait(s, 0)
        total = pair_sum(s, y, z) + from_y[s, 0].astype(jnp.float32)
        for k in range(depth - 1):
            block = from_z.at[s, k]
            remote(block, block, rz_s.at[s, k], rz_r.at[s, k], y_peer).wait_recv()
            total = total + from_z[s, k].astype(jnp.float32)
        h = (x_ref[batch] if layer == 0 else out_ref[layer - 1, batch]).astype(jnp.float32)
        out_ref[layer, batch] = (h + total * 0.125).astype(jnp.bfloat16)

    norm_send(0, 0)
    gather_z_done(0, 0)
    norm_send(0, 1)
    gather_y_done(0, 0)
    gather_core_done(0, 0)
    gather_z_done(0, 1)
    compute(0, 0)
    sum_core(0, 0)
    gather_y_done(0, 1)
    gather_core_done(0, 1)
    sum_y(0, 0)
    compute(0, 1)
    sum_core(0, 1)
    sum_z(0, 0)
    sum_y(0, 1)
    finish(0, 0)
    norm_send(1, 0)
    sum_z(0, 1)
    gather_z_done(1, 0)
    finish(0, 1)
    norm_send(1, 1)
    gather_y_done(1, 0)
    gather_core_done(1, 0)
    gather_z_done(1, 1)
    compute(1, 0)
    sum_core(1, 0)
    gather_y_done(1, 1)
    gather_core_done(1, 1)
    sum_y(1, 0)
    compute(1, 1)
    sum_core(1, 1)
    sum_z(1, 0)
    sum_y(1, 1)
    finish(1, 0)
    sum_z(1, 1)
    finish(1, 1)

    for copy in sends:
        copy.wait_send()


def fused_on_device(count, inputs, routes, norm_gain, w_gate_up, w_down):
    batches, tokens, features = inputs.shape
    layers = routes.shape[0]
    units = w_down.shape[2]
    slots = layers * batches
    depth = count // (PAIR * PAIR)
    bf16 = jnp.bfloat16
    vmem = pl.BlockSpec(memory_space=pltpu.VMEM)
    hbm = pl.BlockSpec(memory_space=pl.ANY)
    dma = pltpu.SemaphoreType.DMA
    short = max(depth - 1, 1)
    return pl.pallas_call(
        functools.partial(moe_kernel, count),
        out_shape=jax.ShapeDtypeStruct((layers, batches, tokens, features), bf16),
        in_specs=[vmem, vmem, vmem, hbm, hbm],
        out_specs=vmem,
        scratch_shapes=[
            pltpu.VMEM((layers, features, 2 * units), bf16),
            pltpu.VMEM((layers, units, features), bf16),
            pltpu.VMEM((slots, PAIR, PAIR, depth, tokens, features + LANES), bf16),
            pltpu.VMEM((count * tokens, units), bf16),
            pltpu.VMEM((slots, PAIR, PAIR, depth, tokens, features), bf16),
            pltpu.VMEM((slots, PAIR, depth, tokens, features), bf16),
            pltpu.VMEM((slots, depth, tokens, features), bf16),
            pltpu.VMEM((slots, depth, tokens, features), bf16),
            pltpu.VMEM((slots, short, tokens, features), bf16),
            pltpu.VMEM((slots, short, tokens, features), bf16),
            dma((layers, 2)),
            dma((slots, short)),
            dma((slots, short)),
            dma((slots, depth)),
            dma((slots, depth)),
            dma((slots, PAIR * depth)),
            dma((slots, PAIR * depth)),
            dma((slots, 2)),
            dma((slots, 2)),
            dma((slots, depth)),
            dma((slots, depth)),
            dma((slots, short)),
            dma((slots, short)),
        ],
        compiler_params=pltpu.CompilerParams(
            collective_id=0, has_side_effects=True, vmem_limit_bytes=60 << 20
        ),
        name="moe",
    )(inputs, routes, norm_gain, w_gate_up, w_down)


def solution(mesh):
    placed = (
        P(None, ("groups", "expert"), None),
        P("section", None, ("groups", "expert"), None),
        P("section", None),
        P("section", "expert", None, None),
        P("section", "expert", None, None),
    )
    count = mesh.shape["expert"]
    fused = mesh.shape["section"] == 1 and count % (PAIR * PAIR) == 0 and PAIR * PAIR < count <= LANES
    return jax.shard_map(
        functools.partial(fused_on_device, count) if fused else on_device,
        mesh=mesh,
        in_specs=placed,
        out_specs=P("section", None, ("groups", "expert"), None),
        check_vma=False,
    )
```

```python
import functools

import jax
import jax.numpy as jnp
from jax import lax
from jax.experimental import pallas as pl
from jax.experimental.pallas import tpu as pltpu
from jax.sharding import PartitionSpec as P

eps = 1e-06


def from_behind(value, axis, steps):
    count = lax.axis_size(axis)
    initial, last = (max(0, -steps), min(count, count - steps))
    return lax.ppermute(value, axis, [(source, source + steps) for source in range(initial, last)])


def expert_rows(rows, gate_up, down_proj):
    hidden_size = down_proj.shape[0]
    joined = jnp.dot(rows, gate_up, preferred_element_type=jnp.float32)
    hidden = (jax.nn.silu(joined[:, :hidden_size]) * joined[:, hidden_size:]).astype(jnp.bfloat16)
    return jnp.dot(hidden, down_proj, preferred_element_type=jnp.float32).astype(jnp.bfloat16)


def run_experts(received, gate_up, down_proj):
    flat = received.reshape(-1, received.shape[2])
    done = expert_rows(flat, gate_up, down_proj)
    return done.reshape(received.shape)


def moe_layer(current, layer_routes, gain_row, gate_up, down_proj, experts, capacity):
    tokens, features = current.shape
    widened = current.astype(jnp.float32)
    scale_inv = lax.rsqrt(jnp.mean(widened * widened, axis=-1, keepdims=True) + eps)
    normed = (widened * scale_inv * gain_row).astype(jnp.bfloat16)
    expert_ids = jnp.arange(experts, dtype=jnp.int32)
    onehot = (layer_routes[:, :, None] == expert_ids[None, None, :]).astype(jnp.int32)
    counted = jnp.sum(onehot, axis=1)
    before = jnp.cumsum(counted, axis=0) - counted
    slot_of = jnp.sum(onehot * (expert_ids[None, None, :] * capacity + before[:, None, :]), axis=2)
    slot_ids = jnp.arange(experts * capacity, dtype=jnp.int32)
    placing = jnp.sum(
        (slot_ids[:, None, None] == slot_of[None, :, :]).astype(jnp.int32), axis=2
    ).astype(jnp.bfloat16)
    outgoing = jnp.dot(placing, normed, preferred_element_type=jnp.float32).astype(jnp.bfloat16)
    outgoing = outgoing.reshape(experts, capacity, features)
    results = run_experts(
        lax.all_to_all(outgoing, "expert", split_axis=0, concat_axis=0, tiled=True),
        gate_up,
        down_proj,
    )
    returned = lax.all_to_all(results, "expert", split_axis=0, concat_axis=0, tiled=True).reshape(
        experts * capacity, features
    )
    combined = (
        jnp.einsum("it,id->td", placing, returned, preferred_element_type=jnp.float32) * 0.125
    )
    return (widened + combined).astype(jnp.bfloat16)


def on_device(inputs, routes, norm_gain, w_gate_up, w_down):
    experts = lax.axis_size("expert")
    sections = lax.axis_size("section")
    batches, tokens, features = inputs.shape
    top_k = routes.shape[3]
    capacity = min(tokens, 2 * tokens * top_k // experts)
    if sections == 1:
        layers_out = []
        previous = [inputs[batch_no] for batch_no in range(batches)]
        for layer_no in range(routes.shape[0]):
            current_layer = []
            for batch_no in range(batches):
                current_layer.append(
                    moe_layer(
                        previous[batch_no],
                        routes[layer_no, batch_no],
                        norm_gain[layer_no],
                        w_gate_up[layer_no, 0],
                        w_down[layer_no, 0],
                        experts,
                        capacity,
                    )
                )
            layers_out.append(jnp.stack(current_layer))
            previous = current_layer
        return jnp.stack(layers_out)
    segment_no = lax.axis_index("section")
    layer_routes = routes[0]
    gain_row = norm_gain[0]
    gate_up = w_gate_up[0, 0]
    down_proj = w_down[0, 0]
    handed = jnp.zeros((tokens, features), jnp.bfloat16)
    finished = []
    for turn_no in range(batches + 1):
        if turn_no < batches:
            fresh_rows = inputs[turn_no]
        else:
            fresh_rows = jnp.zeros((tokens, features), jnp.bfloat16)
        current = jnp.where(segment_no == 0, fresh_rows, handed)
        batch_pick = jnp.clip(turn_no - segment_no, 0, batches - 1)
        turn_routes = lax.dynamic_index_in_dim(layer_routes, batch_pick, 0, keepdims=False)
        result = moe_layer(current, turn_routes, gain_row, gate_up, down_proj, experts, capacity)
        finished.append(result)
        if turn_no < batches:
            handed = from_behind(result, "section", 1)
    first_segment = jnp.stack(finished[:batches])
    second_segment = jnp.stack(finished[1:])
    return jnp.where(segment_no == 0, first_segment, second_segment)[None]

LANES = 128
PAIR = 2
TILE = 256


def flat_rows(block):
    return block.reshape(-1, block.shape[-1])


def moe_kernel(
    count,
    x_ref,
    routes_ref,
    gain_ref,
    gu_hbm,
    down_hbm,
    out_ref,
    gu,
    down,
    rows,
    hidden,
    made,
    from_core,
    to_y,
    from_y,
    to_z,
    from_z,
    w_sem,
    az_s,
    az_r,
    ay_s,
    ay_r,
    ac_s,
    ac_r,
    rc_s,
    rc_r,
    ry_s,
    ry_r,
    rz_s,
    rz_r,
):
    layers, batches = routes_ref.shape[0], routes_ref.shape[1]
    tokens, features = x_ref.shape[1], x_ref.shape[2]
    units = down.shape[1]
    depth = count // (PAIR * PAIR)
    me = lax.axis_index("expert")
    c = lax.rem(me, PAIR)
    y = lax.rem(lax.div(me, PAIR), PAIR)
    z = lax.div(me, PAIR * PAIR)
    other_c, other_y = 1 - c, 1 - y

    def expert_at(zz, yy, cc):
        return (zz * PAIR + yy) * PAIR + cc

    def z_up(k):
        return lax.rem(z + k, depth)

    core_peer = expert_at(z, y, other_c)
    y_peer = expert_at(z, other_y, c)

    def remote(src, dst, send, recv, target):
        return pltpu.make_async_remote_copy(
            src_ref=src,
            dst_ref=dst,
            send_sem=send,
            recv_sem=recv,
            device_id={"expert": target},
            device_id_type=pl.DeviceIdType.MESH,
        )

    loads = []
    for layer in range(layers):
        for number, (source, target) in enumerate(((gu_hbm, gu), (down_hbm, down))):
            load = pltpu.make_async_copy(
                source.at[layer, 0], target.at[layer], w_sem.at[layer, number]
            )
            load.start()
            loads.append(load)

    barrier = pltpu.get_barrier_semaphore()
    for peer in [expert_at(z_up(k), y, c) for k in range(1, depth)] + [core_peer, y_peer]:
        pl.semaphore_signal(
            barrier, inc=1, device_id={"expert": peer}, device_id_type=pl.DeviceIdType.MESH
        )
    pl.semaphore_wait(barrier, depth + 1)

    sends = []

    def go(copy):
        copy.start()
        sends.append(copy)

    def slot(layer, batch):
        return layer * batches + batch

    def nearest(n):
        chosen = z * 0
        for at in range(depth):
            ranked = sorted(range(depth), key=lambda v: (abs(v - at), v))
            chosen = jnp.where(z == at, ranked[n], chosen)
        return chosen

    near = [z] + [nearest(n) for n in range(1, depth)]

    def row_block(s, cc, yy, zz):
        if s == 0:
            return rows.at[s, cc, yy, zz]
        return rows.at[s, cc, yy, zz, :, pl.ds(0, features)]

    def gather_core(s, cc, yy, zz):
        block = row_block(s, cc, yy, zz)
        return remote(block, block, ac_s.at[s, yy, zz], ac_r.at[s, yy, zz], core_peer)

    def gather_y(s, yy, zz):
        block = row_block(s, c, yy, zz)
        return remote(block, block, ay_s.at[s, zz], ay_r.at[s, zz], y_peer)

    def norm_send(layer, batch):
        s = slot(layer, batch)
        h = (x_ref[batch] if layer == 0 else out_ref[layer - 1, batch]).astype(jnp.float32)
        scale = lax.rsqrt(jnp.mean(h * h, axis=-1, keepdims=True) + eps)
        normed = (h * scale * gain_ref[pl.ds(layer, 1), :]).astype(jnp.bfloat16)
        rows[s, c, y, z, :, pl.ds(0, features)] = normed
        if s == 0:
            lanes = lax.broadcasted_iota(jnp.int32, (tokens, LANES), 1)
            named = jnp.zeros((tokens, LANES), jnp.float32)
            for lay in range(layers):
                for bat in range(batches):
                    chosen = routes_ref[lay, bat] + slot(lay, bat) * count
                    for k in range(chosen.shape[1]):
                        named = named + (chosen[:, k : k + 1] == lanes).astype(jnp.float32)
            rows[s, c, y, z, :, pl.ds(features, LANES)] = named.astype(jnp.bfloat16)
        block = row_block(s, c, y, z)
        for n in range(1, depth):
            go(remote(block, block, az_s.at[s, near[n]], az_r.at[s, z], expert_at(near[n], y, c)))
        go(gather_y(s, y, z))
        go(gather_core(s, c, y, z))

    def gather_z_step(layer, batch, n):
        s = slot(layer, batch)
        zz = near[n]
        block = row_block(s, c, y, zz)
        remote(block, block, az_s.at[s, zz], az_r.at[s, zz], y_peer).wait_recv()
        go(gather_y(s, y, zz))
        go(gather_core(s, c, y, zz))

    def gather_y_step(layer, batch, n):
        s = slot(layer, batch)
        gather_y(s, other_y, near[n]).wait_recv()
        go(gather_core(s, c, other_y, near[n]))

    def gather_core_done(layer, batch):
        s = slot(layer, batch)
        for yy in (y, other_y):
            for n in range(depth):
                gather_core(s, other_c, yy, near[n]).wait_recv()

    def compute(layer, batch, jobs):
        s = slot(layer, batch)
        if batch == 0:
            for load in loads[layer * 2 : layer * 2 + 2]:
                load.wait()
        named = flat_rows(rows[0, :, :, :, :, pl.ds(features, LANES)]).astype(jnp.float32)
        lanes = lax.broadcasted_iota(jnp.int32, named.shape, 1)
        mine = jnp.sum(jnp.where(lanes == me + s * count, named, 0.0), axis=1, keepdims=True) > 0.5
        ups, downs = units // TILE, features // TILE
        points = ups + 2

        def run_jobs(point):
            for number, job in enumerate(jobs):
                if number * points // len(jobs) == point:
                    job()

        for j in range(ups):
            x = flat_rows(rows[s, :, :, :, :, pl.ds(0, features)])
            gate = jnp.dot(
                x, gu[layer, :, pl.ds(j * TILE, TILE)], preferred_element_type=jnp.float32
            )
            up = jnp.dot(
                x, gu[layer, :, pl.ds(units + j * TILE, TILE)], preferred_element_type=jnp.float32
            )
            value = gate / (1.0 + jnp.exp(-gate)) * up
            hidden[:, pl.ds(j * TILE, TILE)] = jnp.where(mine, value, 0.0).astype(jnp.bfloat16)
            run_jobs(j)

        def down_tile(j, carry):
            cols = pl.ds(pl.multiple_of(j * TILE, TILE), TILE)
            result = jnp.dot(hidden[...], down[layer, :, cols], preferred_element_type=jnp.float32)
            made[s, :, :, :, :, cols] = result.astype(jnp.bfloat16).reshape(
                PAIR, PAIR, depth, tokens, TILE
            )
            return carry

        lax.fori_loop(0, downs // 2, down_tile, 0)
        run_jobs(ups)
        lax.fori_loop(downs // 2, downs, down_tile, 0)
        run_jobs(ups + 1)

    def sum_core_copy(s, cc, yy):
        return remote(
            made.at[s, cc, yy], from_core.at[s, yy], rc_s.at[s, yy], rc_r.at[s, yy], core_peer
        )

    def sum_core(layer, batch):
        s = slot(layer, batch)
        go(sum_core_copy(s, other_c, other_y))
        go(sum_core_copy(s, other_c, y))

    def pair_sum(s, yy, zz):
        return made[s, c, yy, zz].astype(jnp.float32) + from_core[s, yy, zz].astype(jnp.float32)

    def sum_y_copy(s, zz):
        return remote(to_y.at[s, zz], from_y.at[s, zz], ry_s.at[s, zz], ry_r.at[s, zz], y_peer)

    def sum_y(layer, batch):
        s = slot(layer, batch)
        sum_core_copy(s, other_c, other_y).wait_recv()
        for n in reversed(range(depth)):
            zz = near[n]
            to_y[s, zz] = pair_sum(s, other_y, zz).astype(jnp.bfloat16)
            go(sum_y_copy(s, zz))
        sum_core_copy(s, other_c, y).wait_recv()

    def sum_z_step(layer, batch, n):
        s = slot(layer, batch)
        zz = near[n]
        sum_y_copy(s, zz).wait_recv()
        total = pair_sum(s, y, zz) + from_y[s, zz].astype(jnp.float32)
        to_z[s, zz] = total.astype(jnp.bfloat16)
        go(
            remote(
                to_z.at[s, zz], from_z.at[s, z], rz_s.at[s, zz], rz_r.at[s, z], expert_at(zz, y, c)
            )
        )

    def finish(layer, batch):
        s = slot(layer, batch)
        sum_y_copy(s, z).wait_recv()
        total = pair_sum(s, y, z) + from_y[s, z].astype(jnp.float32)
        for n in range(1, depth):
            zz = near[n]
            block = from_z.at[s, zz]
            remote(block, block, rz_s.at[s, zz], rz_r.at[s, zz], y_peer).wait_recv()
            total = total + from_z[s, zz].astype(jnp.float32)
        h = (x_ref[batch] if layer == 0 else out_ref[layer - 1, batch]).astype(jnp.float32)
        out_ref[layer, batch] = (h + total * 0.125).astype(jnp.bfloat16)

    def job(step, layer, batch, n=None):
        if n is None:
            return functools.partial(step, layer, batch)
        return functools.partial(step, layer, batch, n)

    def jobs_of(step, layer, batch, first):
        return [job(step, layer, batch, n) for n in range(first, depth)]

    def run(jobs):
        for one in jobs:
            one()

    def mixed(left, right):
        together = []
        for number in range(max(len(left), len(right))):
            together += left[number : number + 1] + right[number : number + 1]
        return together

    norm_send(0, 0)
    run(jobs_of(gather_z_step, 0, 0, 1))
    norm_send(0, 1)
    run(jobs_of(gather_y_step, 0, 0, 0))
    for layer in range(layers):
        gather_core_done(layer, 0)
        compute(
            layer,
            0,
            jobs_of(gather_z_step, layer, 1, 1) + jobs_of(gather_y_step, layer, 1, 0)[:2],
        )
        sum_core(layer, 0)
        sum_y(layer, 0)
        run(jobs_of(gather_y_step, layer, 1, 2))
        gather_core_done(layer, 1)
        compute(layer, 1, list(reversed(jobs_of(sum_z_step, layer, 0, 1))))
        sum_core(layer, 1)
        finish(layer, 0)
        if layer + 1 < layers:
            norm_send(layer + 1, 0)
        sum_y(layer, 1)
        later = list(reversed(jobs_of(sum_z_step, layer, 1, 1)))
        if layer + 1 < layers:
            run(mixed(later, jobs_of(gather_z_step, layer + 1, 0, 1)))
            gather_y_step(layer + 1, 0, 0)
            finish(layer, 1)
            norm_send(layer + 1, 1)
            run(jobs_of(gather_y_step, layer + 1, 0, 1))
        else:
            run(later)
            finish(layer, 1)

    for copy in sends:
        copy.wait_send()


def fused_on_device(count, inputs, routes, norm_gain, w_gate_up, w_down):
    batches, tokens, features = inputs.shape
    layers = routes.shape[0]
    units = w_down.shape[2]
    slots = layers * batches
    depth = count // (PAIR * PAIR)
    bf16 = jnp.bfloat16
    vmem = pl.BlockSpec(memory_space=pltpu.VMEM)
    hbm = pl.BlockSpec(memory_space=pl.ANY)
    dma = pltpu.SemaphoreType.DMA
    return pl.pallas_call(
        functools.partial(moe_kernel, count),
        out_shape=jax.ShapeDtypeStruct((layers, batches, tokens, features), bf16),
        in_specs=[vmem, vmem, vmem, hbm, hbm],
        out_specs=vmem,
        scratch_shapes=[
            pltpu.VMEM((layers, features, 2 * units), bf16),
            pltpu.VMEM((layers, units, features), bf16),
            pltpu.VMEM((slots, PAIR, PAIR, depth, tokens, features + LANES), bf16),
            pltpu.VMEM((count * tokens, units), bf16),
            pltpu.VMEM((slots, PAIR, PAIR, depth, tokens, features), bf16),
            pltpu.VMEM((slots, PAIR, depth, tokens, features), bf16),
            pltpu.VMEM((slots, depth, tokens, features), bf16),
            pltpu.VMEM((slots, depth, tokens, features), bf16),
            pltpu.VMEM((slots, depth, tokens, features), bf16),
            pltpu.VMEM((slots, depth, tokens, features), bf16),
            dma((layers, 2)),
            dma((slots, depth)),
            dma((slots, depth)),
            dma((slots, depth)),
            dma((slots, depth)),
            dma((slots, PAIR, depth)),
            dma((slots, PAIR, depth)),
            dma((slots, PAIR)),
            dma((slots, PAIR)),
            dma((slots, depth)),
            dma((slots, depth)),
            dma((slots, depth)),
            dma((slots, depth)),
        ],
        compiler_params=pltpu.CompilerParams(
            collective_id=0, has_side_effects=True, vmem_limit_bytes=60 << 20
        ),
        name="moe",
    )(inputs, routes, norm_gain, w_gate_up, w_down)


def choose(count, inputs, routes, norm_gain, w_gate_up, w_down):
    batches, tokens, features = inputs.shape
    layers = routes.shape[0]
    fits = layers == 2 and batches == 2 and layers * batches * count <= LANES
    tiled = w_down.shape[2] % TILE == 0 and features % (2 * TILE) == 0 and tokens % 16 == 0
    run = functools.partial(fused_on_device, count) if fits and tiled else on_device
    return run(inputs, routes, norm_gain, w_gate_up, w_down)


def solution(mesh):
    placed = (
        P(None, ("groups", "expert"), None),
        P("section", None, ("groups", "expert"), None),
        P("section", None),
        P("section", "expert", None, None),
        P("section", "expert", None, None),
    )
    count = mesh.shape["expert"]
    fused = mesh.shape["section"] == 1 and count % (PAIR * PAIR) == 0 and PAIR * PAIR < count
    return jax.shard_map(
        functools.partial(choose, count) if fused else on_device,
        mesh=mesh,
        in_specs=placed,
        out_specs=P("section", None, ("groups", "expert"), None),
        check_vma=False,
    )
```
